32 devices in a mesh: row: 2 (over y), col: 4 (over z), freq: 4 (over x, core).
Axes of the slice: x: 2, y: 2, z: 4, core: 2. Of those that a mesh axis runs over, the one named last changes fastest.
Arguments:
- signal: bfloat16 [4096, 16896], P(('row', 'col')), may hold values from -6 to 6
- starts: int32 [32], replicated, may hold values from 0 to 15872
- win_len: int32 [32], replicated, may hold values from 512 to 1024, as said below
- chan_factor: bfloat16 [4096, 32], P(('row', 'col')), may hold values from -0.375 to 0.375
- freq_factor: bfloat16 [512, 32], P('freq'), may hold values from -2.1213203 to 2.1213203
Outputs:
- new_chan: float32 [4096, 32], P(('row', 'col'))
- new_freq: float32 [512, 32], P('freq')
The draws below stay inside these ranges and needn't reach their ends.
Inputs may be any that keep to these rules, and one draw needn't show every extreme that they name: Each segment's window covers its first win_len samples; in every draw some segment's window spans all 1024 samples.
All inputs are finite; a program needn't handle non-finite values.
Results may differ from the reference program's by a relative error of at most 0.0055.
Values may be sent and summed in bfloat16 or wider, within the bound.
No kernel may reach another device: no remote copies, remote signals or barrier semaphores. Data moves between devices by JAX's collectives and lax.ppermute only.
A program may use at most 128 MiB of HBM per device.

```python
import jax
import jax.numpy as jnp
from jax import lax

C = 4096
F = 512
NW = 1024
R = 32
SEGS = 32
SAMPLES = 16896


def rising_rows(key, rows, cols, fan):
    keys = jax.random.split(key, 2)
    place = (jnp.arange(rows, dtype=jnp.float32)[:, None] + jax.random.uniform(keys[1], (rows, 1), jnp.float32)) / rows
    scaling = 0.2 * jnp.power(10.0, place) / jnp.sqrt(jnp.float32(fan))
    spread = jnp.clip(jax.random.normal(keys[0], (rows, cols), jnp.float32), -6.0, 6.0)
    return spread * scaling


def draw_chan_factor(key, part):
    return rising_rows(jax.random.fold_in(key, 11), C, R, 4 * C).astype(jnp.bfloat16)


def draw_freq_factor(key, part):
    return rising_rows(jax.random.fold_in(key, 23), F, R, F).astype(jnp.bfloat16)


def draw_win_len(key, part):
    keys = jax.random.split(jax.random.fold_in(key, 37), 2)
    lengths = jax.random.randint(keys[0], (SEGS,), NW // 2, NW + 1)
    chosen = jax.random.randint(keys[1], (), 0, SEGS)
    return jnp.where(jnp.arange(SEGS) == chosen, NW, lengths).astype(jnp.int32)


def place_ends(result, key, least, top_value):
    longest = result.shape.index(max(result.shape))
    spots = []
    for shift in (0, 1):
        where = [jax.random.randint(jax.random.fold_in(key, axis), (), 0, length) for axis, length in enumerate(result.shape)]
        where[longest] = (where[longest] + shift) % result.shape[longest]
        spots.append(tuple(where))
    return result.at[spots[0]].set(least).at[spots[1]].set(top_value)


def shard_levels(own_key, dims, shards, least, top_value):
    factor_of = 1.0
    for axis_at, parts in shards:
        heights = jax.random.uniform(jax.random.fold_in(jax.random.fold_in(own_key, 6), axis_at), (parts,), jnp.float32, least / len(shards), top_value / len(shards))
        factor_of = factor_of * jnp.repeat(jnp.exp(heights), dims[axis_at] // parts).reshape((-1,) + (1,) * (len(dims) - 1 - axis_at))
    return factor_of


def bell_draw(own_key, extent, scale, bound, pieces=(), held_as=jnp.bfloat16):
    entries = scale * jax.random.normal(own_key, extent, jnp.float32)
    if pieces:
        entries = entries * shard_levels(own_key, extent, pieces, -0.22, 0.18)
    return jnp.clip(entries, -bound, bound).astype(held_as)


def setup_inputs(seed: int = 0) -> dict:
    arg_keys = jax.random.split(jax.random.key(seed), 6)
    return {
        "signal": bell_draw(arg_keys[0], (C, SAMPLES), 1.0, 6.0, ((0, 8),)),
        "starts": place_ends(jax.random.randint(arg_keys[1], (SEGS,), 0, SAMPLES - NW + 1), jax.random.fold_in(arg_keys[1], 1), 0, SAMPLES - NW).astype(jnp.int32),
        "win_len": draw_win_len(jax.random.fold_in(arg_keys[5], 71), 0),
        "chan_factor": draw_chan_factor(jax.random.fold_in(arg_keys[5], 71), 0),
        "freq_factor": draw_freq_factor(jax.random.fold_in(arg_keys[5], 71), 0),
    }


def fourier_table(start_bin, bin_count):
    position = jnp.arange(NW, dtype=jnp.int32)[:, None]
    frequency = start_bin + jnp.arange(bin_count, dtype=jnp.int32)[None, :]
    phase = (position * frequency % NW).astype(jnp.float32) * (2.0 * jnp.pi / NW)
    return jnp.stack([jnp.cos(phase), -jnp.sin(phase)], axis=1).astype(jnp.bfloat16)

def windowed(signal, starts, win_len):
    position = jnp.arange(NW, dtype=jnp.int32)

    def window_one(start, length):
        portion = lax.dynamic_slice_in_dim(signal, start.astype(jnp.int32), NW, 1).astype(jnp.float32)
        length_float = length.astype(jnp.float32)
        tapering = 0.5 - 0.5 * jnp.cos(2.0 * jnp.pi * position.astype(jnp.float32) / length_float)
        tapering = jnp.where(position < length, tapering, 0.0) / jnp.sqrt(0.375 * length_float)
        return (portion * tapering[None, :]).astype(jnp.bfloat16)
    return jax.vmap(window_one)(starts, win_len)

def solve_gram(system, contracted):
    factor_low = jnp.linalg.cholesky(system)
    middle = lax.linalg.triangular_solve(factor_low, contracted, left_side=False, lower=True, transpose_a=True)
    return lax.linalg.triangular_solve(factor_low, middle, left_side=False, lower=True, transpose_a=False)

def reference(signal, starts, win_len, chan_factor, freq_factor):
    block_rows = min(C, 256)
    block_count = C // block_rows
    transform = fourier_table(0, F).reshape(NW, 2 * F)

    def spectra_block(channel_block):
        segments = windowed(channel_block, starts, win_len)
        product = jnp.dot(segments.reshape(SEGS * block_rows, NW).astype(jnp.float32), transform.astype(jnp.float32), preferred_element_type=jnp.float32)
        return product.astype(jnp.bfloat16).reshape(SEGS, block_rows, 2, F)
    spectra = lax.map(spectra_block, signal.reshape(block_count, block_rows, SAMPLES))

    def add_sums(running, operand_pair):
        spec_block, fac_block = operand_pair
        update = jnp.einsum('kczf,cr->kzrf', spec_block.astype(jnp.float32), fac_block.astype(jnp.float32), precision=lax.Precision.HIGHEST)
        return (running + update, None)
    zeros = jnp.zeros((SEGS, 2, R, F), jnp.float32)
    summed, _ = lax.scan(add_sums, zeros, (spectra, chan_factor.reshape(block_count, block_rows, R)))
    gram_b = jnp.dot(chan_factor.T.astype(jnp.float32), chan_factor.astype(jnp.float32), preferred_element_type=jnp.float32)
    gram_w = jnp.dot(freq_factor.T.astype(jnp.float32), freq_factor.astype(jnp.float32), preferred_element_type=jnp.float32)
    weighted = (summed * freq_factor.T.astype(jnp.float32)[None, None] / SEGS).astype(jnp.bfloat16)

    def contract_block(spec_block):
        return jnp.einsum('kczf,kzrf->cr', spec_block.astype(jnp.float32), weighted.astype(jnp.float32), precision=lax.Precision.HIGHEST)
    contracted = lax.map(contract_block, spectra).reshape(C, R)
    new_chan = solve_gram(gram_b * gram_w, contracted)
    rounded = new_chan.astype(jnp.bfloat16).reshape(block_count, block_rows, R)
    images, _ = lax.scan(add_sums, zeros, (spectra, rounded))
    gram_a = jnp.dot(new_chan.T, new_chan, precision=lax.Precision.HIGHEST)
    freq_terms = jnp.einsum('kzrf,kzrf->fr', images, summed, precision=lax.Precision.HIGHEST) / SEGS
    new_freq = solve_gram(gram_a * gram_b, freq_terms)
    return (new_chan, new_freq)
```

```python
import jax
import jax.numpy as jnp
import numpy as np
from jax import lax
from jax.experimental import pallas as pl
from jax.experimental.pallas import tpu as pltpu
from jax.sharding import PartitionSpec as P

NW = 1024
HALF = NW // 2
SEGS = 32
LANES = 128
ALL = ("row", "col", "freq")
F32 = jnp.float32
BF16 = jnp.bfloat16
HIGHEST = lax.Precision.HIGHEST
VMEM_BYTES = 48 << 20


def half_table():
    position = np.arange(HALF)
    phase = (np.outer(position, position) % NW) * (2.0 * np.pi / NW)
    table = np.concatenate([np.cos(phase), -np.sin(phase)], axis=1)
    return jnp.asarray(table.astype(np.float32)).astype(BF16)


def iota(shape, axis):
    return lax.broadcasted_iota(jnp.int32, shape, axis)


def dot(a, b, contract=((1,), (0,)), precision=None):
    return lax.dot_general(
        a, b, (contract, ((), ())), precision=precision, preferred_element_type=F32
    )


def spd_inverse(system):
    size = system.shape[0]
    rows, cols = iota((size, size), 0), iota((size, size), 1)
    for i in range(size):
        row, col = system[i : i + 1, :], system[:, i : i + 1]
        pivot = 1.0 / system[i : i + 1, i : i + 1]
        scaled = row * pivot
        here, there = rows == i, cols == i
        updated = system - col * scaled
        updated = jnp.where(there, col * pivot, updated)
        updated = jnp.where(here, scaled, updated)
        system = jnp.where(here & there, -pivot, updated)
    return -system


def split_rows(gram, size):
    spread = (iota((size, LANES), 1) % size == iota((size, LANES), 0)).astype(F32)
    tiled = dot(gram, spread, precision=HIGHEST)
    high = tiled.astype(BF16).astype(F32)
    return jnp.where(iota((size, LANES), 1) // size % 2 == 0, high, tiled - high)


def join_rows(ref, group):
    value = ref[...]
    value = value + pltpu.roll(value, LANES - 32, 1)
    other = pltpu.roll(value, 64, 1)
    return jnp.where(iota(value.shape, 0) % group < group // 2, value, other)[:, :32]


def packed_side(ref, start, count):
    upper = ref[pl.ds(start, count), :]
    lower = ref[pl.ds(start + count, count), :]
    return jnp.where(iota((count, LANES), 1) < 64, upper, lower)


def taper_of(win_ref):
    length = jnp.zeros((SEGS, LANES), F32)
    which = iota((SEGS, LANES), 0)
    for k in range(SEGS):
        length = jnp.where(which == k, win_ref[k].astype(F32), length)
    norm = 1.0 / (0.375 * length)
    scale = jnp.sqrt(norm)
    pieces = []
    for j in range(NW // LANES):
        position = (iota((SEGS, LANES), 1) + j * LANES).astype(F32)
        angle = jnp.pi * (position / length - 0.5)
        square = angle * angle
        value = 1.0 + square * (
            -1.0 / 2
            + square
            * (
                1.0 / 24
                + square
                * (
                    -1.0 / 720
                    + square
                    * (1.0 / 40320 + square * (-1.0 / 3628800 + square * (1.0 / 479001600)))
                )
            )
        )
        pieces.append(jnp.where(position < length, value * value * scale, 0.0))
    return jnp.concatenate(pieces, axis=1)


def windows(z_ref, y_ref, starts_ref):
    lane = iota((8, LANES), 1)
    for k in range(SEGS):
        start = starts_ref[k]
        major, minor = start // LANES, start % LANES
        mixed = jnp.where(lane >= minor, z_ref[pl.ds(major, 8), :], z_ref[pl.ds(major + 1, 8), :])
        y_ref[k] = pltpu.roll(mixed, (LANES - minor) % LANES, 1)
    return jnp.concatenate([y_ref[:, j, :] for j in range(8)], axis=1)


def forward(samples, table):
    low, high = samples[:, :HALF], samples[:, HALF:]
    both = jnp.concatenate([low + high, low - high], axis=0)
    top = both.astype(BF16)
    rest = (both - top.astype(F32)).astype(BF16)
    out = dot(jnp.concatenate([top, rest], axis=0), table)
    out = out[: 2 * SEGS] + out[2 * SEGS :]
    return jnp.where(iota((SEGS, NW), 1) % 2 == 0, out[:SEGS], out[SEGS:])


def body(signal, starts, win_len, chan_factor, freq_factor):
    mesh_size = {name: lax.axis_size(name) for name in ALL}
    nq = mesh_size["freq"]
    nc = mesh_size["row"] * mesh_size["col"]
    ndev = nq * nc
    chans, samples = signal.shape
    bins, rank = freq_factor.shape
    span = samples // nq
    rows = span // LANES
    total_rows = rows * nq
    freq_row, b_row, w_row = rows, rows + 1, rows + 5
    msg_rows = rows + 7
    chunks = 3
    chunk = span // chunks
    assert rank == 32 and nq == 4 and bins == LANES and ndev >= rank and nc % 8 == 0
    assert span % (chunks * LANES) == 0 and msg_rows % 8 == 0

    vmem = pl.BlockSpec(memory_space=pltpu.VMEM)
    smem = pl.BlockSpec(memory_space=pltpu.SMEM)
    hbm = pl.BlockSpec(memory_space=pl.ANY)
    params = pltpu.CompilerParams(vmem_limit_bytes=VMEM_BYTES)
    table = half_table()
    msg = jax.ShapeDtypeStruct((ndev, msg_rows, LANES), BF16)

    def fetch(signal_ref, buf, sem):
        base = lax.axis_index("freq") * span
        copies = []
        for i in range(chunks):
            where = pl.multiple_of(base + i * chunk, LANES)
            copies.append(
                pltpu.make_async_copy(
                    signal_ref.at[:, pl.ds(where, chunk)], buf.at[i], sem.at[i]
                )
            )
        for copy in copies:
            copy.start()
        return copies

    signal_scratch = [
        pltpu.VMEM((chunks, chans, chunk), BF16),
        pltpu.SemaphoreType.DMA((chunks,)),
    ]

    def channel_sums(lhs, copies, buf, out_ref):
        if ndev > rank:
            out_ref[...] = jnp.zeros_like(out_ref)
        for i in range(chunks):
            copies[i].wait()
            part = dot(lhs, buf[i])
            for j in range(chunk // LANES):
                out_ref[:rank, i * (chunk // LANES) + j, :] = part[:, j * LANES : (j + 1) * LANES]

    def sums_kernel(signal_ref, win_ref, chan_ref, freq_ref, msg_ref, taper_ref, buf, sem, out, gs):
        copies = fetch(signal_ref, buf, sem)
        q = lax.axis_index("freq")
        c = lax.axis_index("row") * mesh_size["col"] + lax.axis_index("col")
        taper_ref[...] = taper_of(win_ref)
        chan = chan_ref[...].astype(F32).T
        chan_low = chan.astype(BF16)
        weights = freq_ref[...].astype(F32).T
        channel_sums(chan_low, copies, buf, out)
        out[:rank, freq_row, :] = weights
        gs[...] = split_rows(dot(chan_low, chan_low, ((1,), (1,))), rank)
        side = packed_side(gs, q * 8, 4)
        out[:, b_row : b_row + 4, :] = jnp.broadcast_to(side[None], (ndev, 4, LANES))
        weights_low = weights.astype(BF16)
        gs[...] = split_rows(dot(weights_low, weights_low, ((1,), (1,))), rank)
        side = packed_side(gs, (c % 8) * 4, 2)
        out[:, w_row : w_row + 2, :] = jnp.broadcast_to(side[None], (ndev, 2, LANES))
        msg_ref[...] = out[...].astype(BF16)

    message, taper = pl.pallas_call(
        sums_kernel,
        out_shape=(msg, jax.ShapeDtypeStruct((SEGS, NW), F32)),
        in_specs=[hbm, smem, vmem, vmem],
        out_specs=(vmem, vmem),
        scratch_shapes=signal_scratch
        + [pltpu.VMEM((ndev, msg_rows, LANES), F32), pltpu.VMEM((rank, LANES), F32)],
        compiler_params=params,
        name="channel_sums",
    )(signal, win_len, chan_factor, freq_factor)
    received = lax.all_to_all(message, ALL, 0, 0, tiled=True)

    z_rows = (total_rows + 8 + 7) // 8 * 8

    def gather_rank(rcv_ref, z_ref, gs):
        for q in range(nq):
            total = rcv_ref[q].astype(F32)
            for c in range(1, nc):
                total = total + rcv_ref[c * nq + q].astype(F32)
            z_ref[q * rows : (q + 1) * rows, :] = total[:rows]
            gs[8 * q : 8 * q + 4, :] = total[b_row : b_row + 4]
            gs[8 * q + 4 : 8 * q + 8, :] = total[b_row : b_row + 4]
        z_ref[total_rows:, :] = jnp.zeros((z_rows - total_rows, LANES), F32)
        return join_rows(gs, 8)

    def weight_kernel(
        rcv_ref, starts_ref, taper_ref, table_ref,
        msg_ref, summed_ref, inverse_ref, gram_ref,
        z_ref, y_ref, gs, u_ref,
    ):
        gram_b = gather_rank(rcv_ref, z_ref, gs)
        gram_ref[...] = gram_b
        for c in range(8):
            side = rcv_ref[c * nq].astype(F32)[w_row : w_row + 2]
            for q in range(1, nq):
                side = side + rcv_ref[c * nq + q].astype(F32)[w_row : w_row + 2]
            gs[4 * c : 4 * c + 2, :] = side
            gs[4 * c + 2 : 4 * c + 4, :] = side
        gram_w = join_rows(gs, 4)
        inverse_ref[...] = spd_inverse(gram_b * gram_w)
        taper = taper_ref[...]
        table = table_ref[...]
        summed = forward(windows(z_ref, y_ref, starts_ref) * taper, table)
        summed_ref[...] = summed
        weight = jnp.concatenate(
            [rcv_ref[q].astype(F32)[freq_row : freq_row + 1] for q in range(nq)] * 2, axis=1
        )
        weighted = summed * weight / SEGS
        even = iota((SEGS, NW), 1) % 2 == 0
        masked = jnp.concatenate(
            [jnp.where(even, weighted, 0.0), jnp.where(even, 0.0, weighted)], axis=0
        ).astype(BF16)
        back = dot(masked[:, :HALF], table[:, :HALF]) + dot(masked[:, HALF:], table[:, HALF:])
        back = jnp.concatenate(
            [back[:SEGS] + back[SEGS:], back[:SEGS] - back[SEGS:]], axis=1
        )
        back = back * taper
        for j in range(8):
            y_ref[:, j, :] = back[:, j * LANES : (j + 1) * LANES]
        u_ref[...] = jnp.zeros_like(u_ref)
        lane = iota((8, LANES), 1)
        for k in range(SEGS):
            start = starts_ref[k]
            major, minor = start // LANES, start % LANES
            turned = pltpu.roll(y_ref[k], minor, 1)
            first = pl.ds(major, 8)
            u_ref[k % 2, first, :] += jnp.where(lane >= minor, turned, 0.0)
            second = pl.ds(major + 1, 8)
            u_ref[k % 2, second, :] += jnp.where(lane < minor, turned, 0.0)
        added = u_ref[0] + u_ref[1]
        pad = jnp.zeros((msg_rows - rows, LANES), F32)
        for q in range(nq):
            piece = jnp.concatenate([added[q * rows : (q + 1) * rows], pad], axis=0).astype(BF16)
            for c in range(nc):
                msg_ref[c * nq + q] = piece

    square = jax.ShapeDtypeStruct((rank, rank), F32)
    message, summed, inverse, gram_b = pl.pallas_call(
        weight_kernel,
        out_shape=(msg, jax.ShapeDtypeStruct((SEGS, NW), F32), square, square),
        in_specs=[vmem, smem, vmem, vmem],
        out_specs=(vmem,) * 4,
        scratch_shapes=[
            pltpu.VMEM((z_rows, LANES), F32),
            pltpu.VMEM((SEGS, 8, LANES), F32),
            pltpu.VMEM((rank, LANES), F32),
            pltpu.VMEM((2, z_rows, LANES), F32),
        ],
        compiler_params=params,
        name="weighting",
    )(received, starts, taper, table)
    received = lax.all_to_all(message, ALL, 0, 0, tiled=True)

    def contract_kernel(signal_ref, rcv_ref, inverse_ref, part_ref, buf, sem, out):
        copies = fetch(signal_ref, buf, sem)
        out[...] = rcv_ref[:rank].astype(F32)
        total = jnp.zeros((rank, chans), F32)
        for i in range(chunks):
            pieces = [out[:, i * (chunk // LANES) + j, :] for j in range(chunk // LANES)]
            operand = jnp.concatenate(pieces, axis=1).astype(BF16)
            copies[i].wait()
            total = total + dot(operand, buf[i], ((1,), (1,)))
        part_ref[...] = dot(inverse_ref[...], total, precision=HIGHEST).astype(BF16)

    part = pl.pallas_call(
        contract_kernel,
        out_shape=jax.ShapeDtypeStruct((rank, chans), BF16),
        in_specs=[hbm, vmem, vmem],
        out_specs=vmem,
        scratch_shapes=signal_scratch + [pltpu.VMEM((rank, msg_rows, LANES), F32)],
        compiler_params=params,
        name="contraction",
    )(signal, received, inverse)
    parts = [part] + [
        lax.ppermute(part, "freq", [(i, i ^ m) for i in range(nq)]) for m in range(1, nq)
    ]

    def images_kernel(signal_ref, p0, p1, p2, p3, chan_ref, msg_ref, buf, sem, out, gs):
        copies = fetch(signal_ref, buf, sem)
        q = lax.axis_index("freq")
        pair = p0[...].astype(F32) + p1[...].astype(F32)
        new_chan = pair + (p2[...].astype(F32) + p3[...].astype(F32))
        chan_ref[...] = new_chan.T
        channel_sums(new_chan.astype(BF16), copies, buf, out)
        gs[...] = split_rows(dot(new_chan, new_chan, ((1,), (1,)), HIGHEST), rank)
        side = packed_side(gs, q * 8, 4)
        out[:, freq_row:, :] = jnp.zeros((ndev, msg_rows - rows, LANES), F32)
        out[:, b_row : b_row + 4, :] = jnp.broadcast_to(side[None], (ndev, 4, LANES))
        msg_ref[...] = out[...].astype(BF16)

    new_chan, message = pl.pallas_call(
        images_kernel,
        out_shape=(jax.ShapeDtypeStruct((chans, rank), F32), msg),
        in_specs=[hbm] + [vmem] * 4,
        out_specs=(vmem, vmem),
        scratch_shapes=signal_scratch
        + [pltpu.VMEM((ndev, msg_rows, LANES), F32), pltpu.VMEM((rank, LANES), F32)],
        compiler_params=params,
        name="image_sums",
    )(signal, *parts)
    received = lax.all_to_all(message, ALL, 0, 0, tiled=True)

    def terms_kernel(
        rcv_ref, starts_ref, taper_ref, table_ref, summed_ref, gram_ref,
        terms_ref, inverse_ref, z_ref, y_ref, gs,
    ):
        gram_a = gather_rank(rcv_ref, z_ref, gs)
        inverse_ref[...] = spd_inverse(gram_a * gram_ref[...])
        images = forward(windows(z_ref, y_ref, starts_ref) * taper_ref[...], table_ref[...])
        terms = jnp.sum(images * summed_ref[...], axis=0, keepdims=True) / SEGS
        terms = terms[:, :HALF] + terms[:, HALF:]
        for d in range(ndev):
            q = d % nq
            terms_ref[d] = terms[:, q * bins : (q + 1) * bins]

    terms, inverse = pl.pallas_call(
        terms_kernel,
        out_shape=(jax.ShapeDtypeStruct((ndev, 1, bins), F32), square),
        in_specs=[vmem, smem, vmem, vmem, vmem, vmem],
        out_specs=(vmem, vmem),
        scratch_shapes=[
            pltpu.VMEM((z_rows, LANES), F32),
            pltpu.VMEM((SEGS, 8, LANES), F32),
            pltpu.VMEM((rank, LANES), F32),
        ],
        compiler_params=params,
        name="frequency_terms",
    )(received, starts, taper, table, summed, gram_b)
    terms = lax.all_to_all(terms, ALL, 0, 0, tiled=True)

    def finish_kernel(terms_ref, inverse_ref, out_ref):
        gathered = terms_ref[:rank, 0, :]
        out_ref[...] = dot(gathered, inverse_ref[...], ((0,), (0,)), HIGHEST)

    new_freq = pl.pallas_call(
        finish_kernel,
        out_shape=jax.ShapeDtypeStruct((bins, rank), F32),
        in_specs=[vmem, vmem],
        out_specs=vmem,
        compiler_params=params,
        name="frequency_solve",
    )(terms, inverse)
    return (new_chan, new_freq)


def solution(mesh):
    return jax.shard_map(
        body,
        mesh=mesh,
        in_specs=(P(("row", "col"), None), P(), P(), P(("row", "col"), None), P("freq", None)),
        out_specs=(P(("row", "col"), None), P("freq", None)),
        check_vma=False,
    )
```

```python
import jax
import jax.numpy as jnp
import numpy as np
from jax import lax
from jax.experimental import pallas as pl
from jax.experimental.pallas import tpu as pltpu
from jax.sharding import PartitionSpec as P

NW = 1024
HALF = NW // 2
SEGS = 32
LANES = 128
ALL = ("row", "col", "freq")
F32 = jnp.float32
BF16 = jnp.bfloat16
HIGHEST = lax.Precision.HIGHEST
VMEM_BYTES = 16 << 20


def half_table():
    position = np.arange(HALF)
    phase = (np.outer(position, position) % NW) * (2.0 * np.pi / NW)
    table = np.concatenate([np.cos(phase), -np.sin(phase)], axis=1)
    return jnp.asarray(table.astype(np.float32)).astype(BF16)


def iota(shape, axis):
    return lax.broadcasted_iota(jnp.int32, shape, axis)


def dot(a, b, contract=((1,), (0,)), precision=None):
    return lax.dot_general(
        a, b, (contract, ((), ())), precision=precision, preferred_element_type=F32
    )


def spd_inverse(system):
    size = system.shape[0]
    rows, cols = iota((size, size), 0), iota((size, size), 1)
    for i in range(size):
        row, col = system[i : i + 1, :], system[:, i : i + 1]
        pivot = 1.0 / system[i : i + 1, i : i + 1]
        scaled = row * pivot
        here, there = rows == i, cols == i
        updated = system - col * scaled
        updated = jnp.where(there, col * pivot, updated)
        updated = jnp.where(here, scaled, updated)
        system = jnp.where(here & there, -pivot, updated)
    return -system


def split_rows(gram, size):
    spread = (iota((size, LANES), 1) % size == iota((size, LANES), 0)).astype(F32)
    tiled = dot(gram, spread, precision=HIGHEST)
    high = tiled.astype(BF16).astype(F32)
    return jnp.where(iota((size, LANES), 1) // size % 2 == 0, high, tiled - high)


def join_rows(ref, group):
    value = ref[...]
    value = value + pltpu.roll(value, LANES - 32, 1)
    other = pltpu.roll(value, 64, 1)
    return jnp.where(iota(value.shape, 0) % group < group // 2, value, other)[:, :32]


def packed_side(ref, start, count):
    upper = ref[pl.ds(start, count), :]
    lower = ref[pl.ds(start + count, count), :]
    return jnp.where(iota((count, LANES), 1) < 64, upper, lower)


def taper_of(win_ref):
    length = jnp.zeros((SEGS, LANES), F32)
    which = iota((SEGS, LANES), 0)
    for k in range(SEGS):
        length = jnp.where(which == k, win_ref[k].astype(F32), length)
    norm = 1.0 / (0.375 * length)
    scale = jnp.sqrt(norm)
    pieces = []
    for j in range(NW // LANES):
        position = (iota((SEGS, LANES), 1) + j * LANES).astype(F32)
        angle = jnp.pi * (position / length - 0.5)
        square = angle * angle
        value = 1.0 + square * (
            -1.0 / 2
            + square
            * (
                1.0 / 24
                + square
                * (
                    -1.0 / 720
                    + square
                    * (1.0 / 40320 + square * (-1.0 / 3628800 + square * (1.0 / 479001600)))
                )
            )
        )
        pieces.append(jnp.where(position < length, value * value * scale, 0.0))
    return jnp.concatenate(pieces, axis=1)


def windows(z_ref, y_ref, starts_ref):
    lane = iota((8, LANES), 1)
    for k in range(SEGS):
        start = starts_ref[k]
        major, minor = start // LANES, start % LANES
        mixed = jnp.where(lane >= minor, z_ref[pl.ds(major, 8), :], z_ref[pl.ds(major + 1, 8), :])
        y_ref[k] = pltpu.roll(mixed, (LANES - minor) % LANES, 1)
    return jnp.concatenate([y_ref[:, j, :] for j in range(8)], axis=1)


def forward(samples, table):
    low, high = samples[:, :HALF], samples[:, HALF:]
    both = jnp.concatenate([low + high, low - high], axis=0)
    top = both.astype(BF16)
    rest = (both - top.astype(F32)).astype(BF16)
    out = dot(jnp.concatenate([top, rest], axis=0), table)
    out = out[: 2 * SEGS] + out[2 * SEGS :]
    return jnp.where(iota((SEGS, NW), 1) % 2 == 0, out[:SEGS], out[SEGS:])


def body(signal, starts, win_len, chan_factor, freq_factor):
    mesh_size = {name: lax.axis_size(name) for name in ALL}
    nq = mesh_size["freq"]
    nc = mesh_size["row"] * mesh_size["col"]
    ndev = nq * nc
    chans, samples = signal.shape
    bins, rank = freq_factor.shape
    span = samples // nq
    rows = span // LANES
    total_rows = rows * nq
    freq_row, b_row, w_row = rows, rows + 1, rows + 5
    msg_rows = rows + 7
    third = rows // 3
    held_spans = [(0, third), (third, third), (2 * third, rows - 2 * third)]
    first_spans = [(i, min(8, rows - i)) for i in range(0, rows, 8)]
    assert rank == 32 and nq == 4 and bins == LANES and ndev >= rank and nc % 8 == 0
    assert span % LANES == 0 and msg_rows % 8 == 0

    vmem = pl.BlockSpec(memory_space=pltpu.VMEM)
    smem = pl.BlockSpec(memory_space=pltpu.SMEM)
    hbm = pl.BlockSpec(memory_space=pltpu.HBM)
    params = pltpu.CompilerParams(vmem_limit_bytes=VMEM_BYTES)
    table = half_table()
    pinned = [
        pltpu.with_memory_space_constraint(x, pltpu.HBM)
        for x in (signal, chan_factor.T, freq_factor.T, win_len)
    ]
    msg = jax.ShapeDtypeStruct((ndev, msg_rows, LANES), BF16)

    def fetch(signal_ref, spans, bufs, sem):
        base = lax.axis_index("freq") * span
        copies = []
        for i, ((first, count), buf) in enumerate(zip(spans, bufs)):
            where = pl.multiple_of(base + first * LANES, LANES)
            source = signal_ref.at[:, pl.ds(where, count * LANES)]
            copies.append(pltpu.make_async_copy(source, buf, sem.at[i]))
        for copy in copies:
            copy.start()
        return copies

    def channel_sums(lhs, spans, bufs, copies, out_ref):
        for i, (first, count) in enumerate(spans):
            if copies is not None:
                copies[i].wait()
            part = dot(lhs, bufs[i][...])
            for j in range(count):
                out_ref[:rank, first + j, :] = part[:, j * LANES : (j + 1) * LANES]

    def sums_kernel(
        signal_ref, chan_hbm, freq_hbm, win_hbm, msg_ref, taper_ref,
        buf, sem, chan_ref, freq_ref, win_ref, small, out, gs,
    ):
        small_copies = [
            pltpu.make_async_copy(chan_hbm, chan_ref, small.at[0]),
            pltpu.make_async_copy(freq_hbm, freq_ref, small.at[1]),
            pltpu.make_async_copy(win_hbm, win_ref, small.at[2]),
        ]
        for copy in small_copies:
            copy.start()
        bufs = [buf.at[:, a * LANES : (a + n) * LANES] for a, n in first_spans]
        copies = fetch(signal_ref, first_spans, bufs, sem)
        q = lax.axis_index("freq")
        c = lax.axis_index("row") * mesh_size["col"] + lax.axis_index("col")
        if ndev > rank:
            out[...] = jnp.zeros_like(out)
        for copy in small_copies:
            copy.wait()
        chan_low = chan_ref[...]
        weights_low = freq_ref[...]
        out[:rank, freq_row, :] = weights_low.astype(F32)
        gs[...] = split_rows(dot(chan_low, chan_low, ((1,), (1,))), rank)
        side = packed_side(gs, q * 8, 4)
        out[:, b_row : b_row + 4, :] = jnp.broadcast_to(side[None], (ndev, 4, LANES))
        gs[...] = split_rows(dot(weights_low, weights_low, ((1,), (1,))), rank)
        side = packed_side(gs, (c % 8) * 4, 2)
        out[:, w_row : w_row + 2, :] = jnp.broadcast_to(side[None], (ndev, 2, LANES))
        taper_ref[...] = taper_of(win_ref)
        channel_sums(chan_low, first_spans, bufs, copies, out)
        msg_ref[...] = out[...].astype(BF16)

    message, taper = pl.pallas_call(
        sums_kernel,
        out_shape=(msg, jax.ShapeDtypeStruct((SEGS, NW), F32)),
        in_specs=[hbm] * 4,
        out_specs=(vmem, vmem),
        scratch_shapes=[
            pltpu.VMEM((chans, span), BF16),
            pltpu.SemaphoreType.DMA((len(first_spans),)),
            pltpu.VMEM((rank, chans), BF16),
            pltpu.VMEM((rank, bins), BF16),
            pltpu.SMEM((SEGS,), jnp.int32),
            pltpu.SemaphoreType.DMA((3,)),
            pltpu.VMEM((ndev, msg_rows, LANES), F32),
            pltpu.VMEM((rank, LANES), F32),
        ],
        compiler_params=params,
        name="channel_sums",
    )(*pinned)

    def hold_kernel(signal_ref, gram_ref, buf0, buf1, inverse_ref, sem):
        copies = fetch(signal_ref, held_spans[:2], (buf0, buf1), sem)
        inverse_ref[...] = spd_inverse(gram_ref[...])
        for copy in copies:
            copy.wait()

    def inverse_kernel(gram_ref, inverse_ref):
        inverse_ref[...] = spd_inverse(gram_ref[...])

    def inverse_of(gram):
        return pl.pallas_call(
            inverse_kernel,
            out_shape=jax.ShapeDtypeStruct(gram.shape, F32),
            in_specs=[vmem],
            out_specs=vmem,
            compiler_params=params,
            name="inverse",
        )(gram)

    received = lax.all_to_all(message, ALL, 0, 0, tiled=True)

    z_rows = (total_rows + 8 + 7) // 8 * 8

    def gather_rank(rcv_ref, z_ref, gs):
        for q in range(nq):
            total = rcv_ref[q].astype(F32)
            for c in range(1, nc):
                total = total + rcv_ref[c * nq + q].astype(F32)
            z_ref[q * rows : (q + 1) * rows, :] = total[:rows]
            gs[8 * q : 8 * q + 4, :] = total[b_row : b_row + 4]
            gs[8 * q + 4 : 8 * q + 8, :] = total[b_row : b_row + 4]
        z_ref[total_rows:, :] = jnp.zeros((z_rows - total_rows, LANES), F32)
        return join_rows(gs, 8)

    def weight_kernel(
        rcv_ref, starts_ref, taper_ref, table_ref,
        msg_ref, summed_ref, system_ref, gram_ref,
        z_ref, y_ref, gs, u_ref,
    ):
        gram_b = gather_rank(rcv_ref, z_ref, gs)
        gram_ref[...] = gram_b
        for c in range(8):
            side = rcv_ref[c * nq].astype(F32)[w_row : w_row + 2]
            for q in range(1, nq):
                side = side + rcv_ref[c * nq + q].astype(F32)[w_row : w_row + 2]
            gs[4 * c : 4 * c + 2, :] = side
            gs[4 * c + 2 : 4 * c + 4, :] = side
        gram_w = join_rows(gs, 4)
        system_ref[...] = gram_b * gram_w
        taper = taper_ref[...]
        table = table_ref[...]
        summed = forward(windows(z_ref, y_ref, starts_ref) * taper, table)
        summed_ref[...] = summed
        weight = jnp.concatenate(
            [rcv_ref[q].astype(F32)[freq_row : freq_row + 1] for q in range(nq)] * 2, axis=1
        )
        weighted = summed * weight / SEGS
        even = iota((SEGS, NW), 1) % 2 == 0
        masked = jnp.concatenate(
            [jnp.where(even, weighted, 0.0), jnp.where(even, 0.0, weighted)], axis=0
        ).astype(BF16)
        back = dot(masked[:, :HALF], table[:, :HALF]) + dot(masked[:, HALF:], table[:, HALF:])
        back = jnp.concatenate(
            [back[:SEGS] + back[SEGS:], back[:SEGS] - back[SEGS:]], axis=1
        )
        back = back * taper
        for j in range(8):
            y_ref[:, j, :] = back[:, j * LANES : (j + 1) * LANES]
        u_ref[...] = jnp.zeros_like(u_ref)
        lane = iota((8, LANES), 1)
        for k in range(SEGS):
            start = starts_ref[k]
            major, minor = start // LANES, start % LANES
            turned = pltpu.roll(y_ref[k], minor, 1)
            first = pl.ds(major, 8)
            u_ref[k % 2, first, :] += jnp.where(lane >= minor, turned, 0.0)
            second = pl.ds(major + 1, 8)
            u_ref[k % 2, second, :] += jnp.where(lane < minor, turned, 0.0)
        added = u_ref[0] + u_ref[1]
        pad = jnp.zeros((msg_rows - rows, LANES), F32)
        for q in range(nq):
            piece = jnp.concatenate([added[q * rows : (q + 1) * rows], pad], axis=0).astype(BF16)
            for c in range(nc):
                msg_ref[c * nq + q] = piece

    square = jax.ShapeDtypeStruct((rank, rank), F32)
    message, summed, system, gram_b = pl.pallas_call(
        weight_kernel,
        out_shape=(msg, jax.ShapeDtypeStruct((SEGS, NW), F32), square, square),
        in_specs=[vmem, smem, vmem, vmem],
        out_specs=(vmem,) * 4,
        scratch_shapes=[
            pltpu.VMEM((z_rows, LANES), F32),
            pltpu.VMEM((SEGS, 8, LANES), F32),
            pltpu.VMEM((rank, LANES), F32),
            pltpu.VMEM((2, z_rows, LANES), F32),
        ],
        compiler_params=params,
        name="weighting",
    )(received, starts, taper, table)
    received = lax.all_to_all(message, ALL, 0, 0, tiled=True)
    pieces = [jax.ShapeDtypeStruct((chans, n * LANES), BF16) for _, n in held_spans]
    *held, inverse = pl.pallas_call(
        hold_kernel,
        out_shape=(pieces[0], pieces[1], square),
        in_specs=[hbm, vmem],
        out_specs=(vmem,) * 3,
        scratch_shapes=[pltpu.SemaphoreType.DMA((2,))],
        compiler_params=params,
        name="hold_signal",
    )(pinned[0], system)

    def contract_kernel(
        signal_ref, buf0, buf1, rcv_ref, inverse_ref, part_ref, buf2, sem, out
    ):
        copies = fetch(signal_ref, held_spans[2:], (buf2,), sem)
        out[...] = rcv_ref[:rank].astype(F32)
        total = jnp.zeros((rank, chans), F32)
        for (first, count), buf in zip(held_spans, (buf0, buf1, buf2)):
            columns = [out[:, first + j, :] for j in range(count)]
            operand = jnp.concatenate(columns, axis=1).astype(BF16)
            if buf is buf2:
                copies[0].wait()
            total = total + dot(operand, buf[...], ((1,), (1,)))
        part_ref[...] = dot(inverse_ref[...], total, precision=HIGHEST).astype(BF16)

    part, last = pl.pallas_call(
        contract_kernel,
        out_shape=(jax.ShapeDtypeStruct((rank, chans), BF16), pieces[2]),
        in_specs=[hbm] + [vmem] * 4,
        out_specs=(vmem, vmem),
        scratch_shapes=[
            pltpu.SemaphoreType.DMA((1,)),
            pltpu.VMEM((rank, msg_rows, LANES), F32),
        ],
        compiler_params=params,
        name="contraction",
    )(pinned[0], *held, received, inverse)
    parts = [part] + [
        lax.ppermute(part, "freq", [(i, i ^ m) for i in range(nq)]) for m in range(1, nq)
    ]

    def images_kernel(buf0, buf1, buf2, p0, p1, p2, p3, chan_ref, msg_ref, out, gs):
        q = lax.axis_index("freq")
        pair = p0[...].astype(F32) + p1[...].astype(F32)
        new_chan = pair + (p2[...].astype(F32) + p3[...].astype(F32))
        chan_ref[...] = new_chan
        if ndev > rank:
            out[...] = jnp.zeros_like(out)
        channel_sums(new_chan.astype(BF16), held_spans, (buf0, buf1, buf2), None, out)
        gs[...] = split_rows(dot(new_chan, new_chan, ((1,), (1,)), HIGHEST), rank)
        side = packed_side(gs, q * 8, 4)
        out[:, freq_row:, :] = jnp.zeros((ndev, msg_rows - rows, LANES), F32)
        out[:, b_row : b_row + 4, :] = jnp.broadcast_to(side[None], (ndev, 4, LANES))
        msg_ref[...] = out[...].astype(BF16)

    new_chan, message = pl.pallas_call(
        images_kernel,
        out_shape=(jax.ShapeDtypeStruct((rank, chans), F32), msg),
        in_specs=[vmem] * 7,
        out_specs=(vmem, vmem),
        scratch_shapes=[pltpu.VMEM((ndev, msg_rows, LANES), F32), pltpu.VMEM((rank, LANES), F32)],
        compiler_params=params,
        name="image_sums",
    )(*held, last, *parts)
    received = lax.all_to_all(message, ALL, 0, 0, tiled=True)

    def terms_kernel(
        rcv_ref, starts_ref, taper_ref, table_ref, summed_ref, gram_ref,
        terms_ref, system_ref, z_ref, y_ref, gs,
    ):
        gram_a = gather_rank(rcv_ref, z_ref, gs)
        system_ref[...] = gram_a * gram_ref[...]
        images = forward(windows(z_ref, y_ref, starts_ref) * taper_ref[...], table_ref[...])
        terms = jnp.sum(images * summed_ref[...], axis=0, keepdims=True) / SEGS
        terms = terms[:, :HALF] + terms[:, HALF:]
        for d in range(ndev):
            q = d % nq
            terms_ref[d] = terms[:, q * bins : (q + 1) * bins]

    terms, system = pl.pallas_call(
        terms_kernel,
        out_shape=(jax.ShapeDtypeStruct((ndev, 1, bins), F32), square),
        in_specs=[vmem, smem, vmem, vmem, vmem, vmem],
        out_specs=(vmem, vmem),
        scratch_shapes=[
            pltpu.VMEM((z_rows, LANES), F32),
            pltpu.VMEM((SEGS, 8, LANES), F32),
            pltpu.VMEM((rank, LANES), F32),
        ],
        compiler_params=params,
        name="frequency_terms",
    )(received, starts, taper, table, summed, gram_b)
    terms = lax.all_to_all(terms, ALL, 0, 0, tiled=True)
    inverse = inverse_of(system)

    def finish_kernel(terms_ref, inverse_ref, out_ref):
        gathered = terms_ref[:rank, 0, :]
        out_ref[...] = dot(inverse_ref[...], gathered, precision=HIGHEST)

    new_freq = pl.pallas_call(
        finish_kernel,
        out_shape=jax.ShapeDtypeStruct((rank, bins), F32),
        in_specs=[vmem, vmem],
        out_specs=vmem,
        compiler_params=params,
        name="frequency_solve",
    )(terms, inverse)
    return (new_chan.T, new_freq.T)


def solution(mesh):
    return jax.shard_map(
        body,
        mesh=mesh,
        in_specs=(P(("row", "col"), None), P(), P(), P(("row", "col"), None), P("freq", None)),
        out_specs=(P(("row", "col"), None), P("freq", None)),
        check_vma=False,
    )
```

```python
import jax
import jax.numpy as jnp
import numpy as np
from jax import lax
from jax.experimental import pallas as pl
from jax.experimental.pallas import tpu as pltpu
from jax.sharding import PartitionSpec as P

NW = 1024
HALF = NW // 2
SEGS = 32
LANES = 128
ALL = ("row", "col", "freq")
F32 = jnp.float32
BF16 = jnp.bfloat16
HIGHEST = lax.Precision.HIGHEST
VMEM_BYTES = 16 << 20
AHEAD = 8


def half_table():
    position = np.arange(HALF)
    phase = (np.outer(position, position) % NW) * (2.0 * np.pi / NW)
    table = np.concatenate([np.cos(phase), -np.sin(phase)], axis=1)
    return jnp.asarray(table.astype(np.float32)).astype(BF16)


def iota(shape, axis):
    return lax.broadcasted_iota(jnp.int32, shape, axis)


def dot(a, b, contract=((1,), (0,)), precision=None):
    return lax.dot_general(
        a, b, (contract, ((), ())), precision=precision, preferred_element_type=F32
    )


def spd_inverse(system):
    size = system.shape[0]
    system = jnp.concatenate([system, jnp.zeros((size, LANES - size), F32)], axis=1)
    rows, cols = iota((size, LANES), 0), iota((size, LANES), 1)
    for i in range(size):
        col = jnp.broadcast_to(system[:, i : i + 1], (size, LANES))
        pivot = 1.0 / col[i : i + 1]
        scaled = jnp.where(cols[:1] == i, pivot, system[i : i + 1] * pivot)
        cleared = jnp.where(cols == i, 0.0, system)
        system = jnp.where(rows == i, scaled, cleared - col * scaled)
    return system[:, :size]


def split_gram(factor, precision=None):
    size = factor.shape[0]
    tiled = dot(factor, jnp.concatenate([factor] * 4, axis=0), ((1,), (1,)), precision)
    high = tiled.astype(BF16).astype(F32)
    return jnp.where(iota((size, LANES), 1) // size % 2 == 0, high, tiled - high)


def join_rows(ref, group):
    value = ref[...]
    value = value + pltpu.roll(value, LANES - 32, 1)
    other = pltpu.roll(value, 64, 1)
    return jnp.where(iota(value.shape, 0) % group < group // 2, value, other)[:, :32]


def packed_side(ref, start, count):
    upper = ref[pl.ds(start, count), :]
    lower = ref[pl.ds(start + count, count), :]
    return jnp.where(iota((count, LANES), 1) < 64, upper, lower)


def taper_of(win_ref):
    length = jnp.zeros((SEGS, LANES), F32)
    which = iota((SEGS, LANES), 0)
    for k in range(SEGS):
        length = jnp.where(which == k, win_ref[k].astype(F32), length)
    norm = 1.0 / (0.375 * length)
    scale = jnp.sqrt(norm)
    pieces = []
    for j in range(NW // LANES):
        position = (iota((SEGS, LANES), 1) + j * LANES).astype(F32)
        angle = jnp.pi * (position / length - 0.5)
        square = angle * angle
        value = 1.0 + square * (
            -1.0 / 2
            + square
            * (
                1.0 / 24
                + square
                * (
                    -1.0 / 720
                    + square
                    * (1.0 / 40320 + square * (-1.0 / 3628800 + square * (1.0 / 479001600)))
                )
            )
        )
        pieces.append(jnp.where(position < length, value * value * scale, 0.0))
    return jnp.concatenate(pieces, axis=1)


def windows(z_ref, y_ref, starts_ref):
    lane = iota((8, LANES), 1)
    for k in range(SEGS):
        start = starts_ref[k]
        major, minor = start // LANES, start % LANES
        mixed = jnp.where(lane >= minor, z_ref[pl.ds(major, 8), :], z_ref[pl.ds(major + 1, 8), :])
        y_ref[k] = pltpu.roll(mixed, (LANES - minor) % LANES, 1)
    return jnp.concatenate([y_ref[:, j, :] for j in range(8)], axis=1)


def forward(samples, table):
    low, high = samples[:, :HALF], samples[:, HALF:]
    both = jnp.concatenate([low + high, low - high], axis=0)
    top = both.astype(BF16)
    rest = (both - top.astype(F32)).astype(BF16)
    out = dot(jnp.concatenate([top, rest], axis=0), table)
    out = out[: 2 * SEGS] + out[2 * SEGS :]
    return jnp.where(iota((SEGS, NW), 1) % 2 == 0, out[:SEGS], out[SEGS:])


def body(signal, starts, win_len, chan_factor, freq_factor):
    mesh_size = {name: lax.axis_size(name) for name in ALL}
    nq = mesh_size["freq"]
    nc = mesh_size["row"] * mesh_size["col"]
    ndev = nq * nc
    chans, samples = signal.shape
    bins, rank = freq_factor.shape
    span = samples // nq
    rows = span // LANES
    total_rows = rows * nq
    freq_row, b_row, w_row = rows, rows + 1, rows + 5
    msg_rows = rows + 7
    third = rows // 3
    held_spans = [(0, third), (third, third), (2 * third, rows - 2 * third)]
    first_spans = [(0, 12), (12, 12), (24, rows - 24)]
    assert rank == 32 and nq == 4 and bins == LANES and ndev >= rank and nc % 8 == 0
    assert span % LANES == 0 and msg_rows % 8 == 0

    vmem = pl.BlockSpec(memory_space=pltpu.VMEM)
    smem = pl.BlockSpec(memory_space=pltpu.SMEM)
    hbm = pl.BlockSpec(memory_space=pltpu.HBM)
    params = pltpu.CompilerParams(vmem_limit_bytes=VMEM_BYTES)
    table = half_table()
    pinned = [
        pltpu.with_memory_space_constraint(x, pltpu.HBM)
        for x in (signal, chan_factor.T, freq_factor.T, win_len)
    ]
    msg = jax.ShapeDtypeStruct((ndev, msg_rows, LANES), BF16)

    def fetch(signal_ref, spans, bufs, sem, ahead=8):
        base = lax.axis_index("freq") * span
        copies = []
        for i, ((first, count), buf) in enumerate(zip(spans, bufs)):
            where = pl.multiple_of(base + first * LANES, LANES)
            source = signal_ref.at[:, pl.ds(where, count * LANES)]
            copies.append(pltpu.make_async_copy(source, buf, sem.at[i]))
        for copy in copies[:ahead]:
            copy.start()
        return copies

    def channel_sums(lhs, spans, bufs, copies, out_ref, ahead=8):
        for i, (first, count) in enumerate(spans):
            if copies[i] is not None:
                copies[i].wait()
                if i + ahead < len(copies):
                    copies[i + ahead].start()
            part = dot(lhs, bufs[i][...])
            for j in range(count):
                out_ref[:rank, first + j, :] = part[:, j * LANES : (j + 1) * LANES]

    def sums_kernel(
        signal_ref, chan_hbm, freq_hbm, win_hbm, msg_ref, taper_ref,
        buf, sem, chan_ref, freq_ref, win_ref, small, out, gs,
    ):
        small_copies = [
            pltpu.make_async_copy(chan_hbm, chan_ref, small.at[0]),
            pltpu.make_async_copy(freq_hbm, freq_ref, small.at[1]),
            pltpu.make_async_copy(win_hbm, win_ref, small.at[2]),
        ]
        for copy in small_copies:
            copy.start()
        bufs = [buf.at[:, a * LANES : (a + n) * LANES] for a, n in first_spans]
        copies = fetch(signal_ref, first_spans, bufs, sem, AHEAD)
        q = lax.axis_index("freq")
        c = lax.axis_index("row") * mesh_size["col"] + lax.axis_index("col")
        if ndev > rank:
            out[...] = jnp.zeros_like(out)
        for copy in small_copies:
            copy.wait()
        taper_ref[...] = taper_of(win_ref)
        chan_low = chan_ref[...]
        weights_low = freq_ref[...]
        out[:rank, freq_row, :] = weights_low.astype(F32)
        gs[0] = split_gram(chan_low)
        gs[1] = split_gram(weights_low)
        channel_sums(chan_low, first_spans, bufs, copies, out, AHEAD)
        side = packed_side(gs.at[0], q * 8, 4)
        out[:, b_row : b_row + 4, :] = jnp.broadcast_to(side[None], (ndev, 4, LANES))
        side = packed_side(gs.at[1], (c % 8) * 4, 2)
        out[:, w_row : w_row + 2, :] = jnp.broadcast_to(side[None], (ndev, 2, LANES))
        msg_ref[...] = out[...].astype(BF16)

    message, taper = pl.pallas_call(
        sums_kernel,
        out_shape=(msg, jax.ShapeDtypeStruct((SEGS, NW), F32)),
        in_specs=[hbm] * 4,
        out_specs=(vmem, vmem),
        scratch_shapes=[
            pltpu.VMEM((chans, span), BF16),
            pltpu.SemaphoreType.DMA((len(first_spans),)),
            pltpu.VMEM((rank, chans), BF16),
            pltpu.VMEM((rank, bins), BF16),
            pltpu.SMEM((SEGS,), jnp.int32),
            pltpu.SemaphoreType.DMA((3,)),
            pltpu.VMEM((ndev, msg_rows, LANES), F32),
            pltpu.VMEM((2, rank, LANES), F32),
        ],
        compiler_params=params,
        name="channel_sums",
    )(*pinned)

    def hold_kernel(signal_ref, gram_ref, buf0, buf1, inverse_ref, sem):
        copies = fetch(signal_ref, held_spans[:2], (buf0, buf1), sem)
        inverse_ref[...] = spd_inverse(gram_ref[...])
        for copy in copies:
            copy.wait()

    def inverse_kernel(gram_ref, inverse_ref):
        inverse_ref[...] = spd_inverse(gram_ref[...])

    def inverse_of(gram):
        return pl.pallas_call(
            inverse_kernel,
            out_shape=jax.ShapeDtypeStruct(gram.shape, F32),
            in_specs=[vmem],
            out_specs=vmem,
            compiler_params=params,
            name="inverse",
        )(gram)

    received = lax.all_to_all(message, ALL, 0, 0, tiled=True)

    z_rows = (total_rows + 8 + 7) // 8 * 8

    def gather_rank(rcv_ref, z_ref, gs):
        for q in range(nq):
            total = rcv_ref[q].astype(F32)
            for c in range(1, nc):
                total = total + rcv_ref[c * nq + q].astype(F32)
            z_ref[q * rows : (q + 1) * rows, :] = total[:rows]
            gs[8 * q : 8 * q + 4, :] = total[b_row : b_row + 4]
            gs[8 * q + 4 : 8 * q + 8, :] = total[b_row : b_row + 4]
        z_ref[total_rows:, :] = jnp.zeros((z_rows - total_rows, LANES), F32)
        return join_rows(gs, 8)

    def weight_kernel(
        rcv_ref, starts_ref, taper_ref, table_ref,
        msg_ref, summed_ref, system_ref, gram_ref,
        z_ref, y_ref, gs, u_ref,
    ):
        gram_b = gather_rank(rcv_ref, z_ref, gs)
        gram_ref[...] = gram_b
        for c in range(8):
            side = rcv_ref[c * nq].astype(F32)[w_row : w_row + 2]
            for q in range(1, nq):
                side = side + rcv_ref[c * nq + q].astype(F32)[w_row : w_row + 2]
            gs[4 * c : 4 * c + 2, :] = side
            gs[4 * c + 2 : 4 * c + 4, :] = side
        gram_w = join_rows(gs, 4)
        system_ref[...] = gram_b * gram_w
        taper = taper_ref[...]
        table = table_ref[...]
        summed = forward(windows(z_ref, y_ref, starts_ref) * taper, table)
        summed_ref[...] = summed
        weight = jnp.concatenate(
            [rcv_ref[q].astype(F32)[freq_row : freq_row + 1] for q in range(nq)] * 2, axis=1
        )
        weighted = summed * weight / SEGS
        even = iota((SEGS, NW), 1) % 2 == 0
        masked = jnp.concatenate(
            [jnp.where(even, weighted, 0.0), jnp.where(even, 0.0, weighted)], axis=0
        ).astype(BF16)
        back = dot(masked[:, :HALF], table[:, :HALF]) + dot(masked[:, HALF:], table[:, HALF:])
        back = jnp.concatenate(
            [back[:SEGS] + back[SEGS:], back[:SEGS] - back[SEGS:]], axis=1
        )
        back = back * taper
        for j in range(8):
            y_ref[:, j, :] = back[:, j * LANES : (j + 1) * LANES]
        u_ref[...] = jnp.zeros_like(u_ref)
        lane = iota((8, LANES), 1)
        for k in range(SEGS):
            start = starts_ref[k]
            major, minor = start // LANES, start % LANES
            turned = pltpu.roll(y_ref[k], minor, 1)
            first = pl.ds(major, 8)
            u_ref[k % 2, first, :] += jnp.where(lane >= minor, turned, 0.0)
            second = pl.ds(major + 1, 8)
            u_ref[k % 2, second, :] += jnp.where(lane < minor, turned, 0.0)
        added = u_ref[0] + u_ref[1]
        pad = jnp.zeros((msg_rows - rows, LANES), F32)
        for q in range(nq):
            piece = jnp.concatenate([added[q * rows : (q + 1) * rows], pad], axis=0).astype(BF16)
            for c in range(nc):
                msg_ref[c * nq + q] = piece

    square = jax.ShapeDtypeStruct((rank, rank), F32)
    message, summed, system, gram_b = pl.pallas_call(
        weight_kernel,
        out_shape=(msg, jax.ShapeDtypeStruct((SEGS, NW), F32), square, square),
        in_specs=[vmem, smem, vmem, vmem],
        out_specs=(vmem,) * 4,
        scratch_shapes=[
            pltpu.VMEM((z_rows, LANES), F32),
            pltpu.VMEM((SEGS, 8, LANES), F32),
            pltpu.VMEM((rank, LANES), F32),
            pltpu.VMEM((2, z_rows, LANES), F32),
        ],
        compiler_params=params,
        name="weighting",
    )(received, starts, taper, table)
    received = lax.all_to_all(message, ALL, 0, 0, tiled=True)
    pieces = [jax.ShapeDtypeStruct((chans, n * LANES), BF16) for _, n in held_spans]
    *held, inverse = pl.pallas_call(
        hold_kernel,
        out_shape=(pieces[0], pieces[1], square),
        in_specs=[hbm, vmem],
        out_specs=(vmem,) * 3,
        scratch_shapes=[pltpu.SemaphoreType.DMA((2,))],
        compiler_params=params,
        name="hold_signal",
    )(pinned[0], system)

    def contract_kernel(
        signal_ref, buf0, buf1, rcv_ref, inverse_ref, part_ref, buf2, sem, out
    ):
        copies = fetch(signal_ref, held_spans[2:], (buf2,), sem)
        out[...] = rcv_ref[:rank].astype(F32)
        total = jnp.zeros((rank, chans), F32)
        for (first, count), buf in zip(held_spans, (buf0, buf1, buf2)):
            columns = [out[:, first + j, :] for j in range(count)]
            operand = jnp.concatenate(columns, axis=1).astype(BF16)
            if buf is buf2:
                copies[0].wait()
            total = total + dot(operand, buf[...], ((1,), (1,)))
        part_ref[...] = dot(inverse_ref[...], total, precision=HIGHEST).astype(BF16)

    part, last = pl.pallas_call(
        contract_kernel,
        out_shape=(jax.ShapeDtypeStruct((rank, chans), BF16), pieces[2]),
        in_specs=[hbm] + [vmem] * 4,
        out_specs=(vmem, vmem),
        scratch_shapes=[
            pltpu.SemaphoreType.DMA((1,)),
            pltpu.VMEM((rank, msg_rows, LANES), F32),
        ],
        compiler_params=params,
        name="contraction",
    )(pinned[0], *held, received, inverse)
    parts = [part] + [
        lax.ppermute(part, "freq", [(i, i ^ m) for i in range(nq)]) for m in range(1, nq)
    ]

    def images_kernel(buf0, buf1, buf2, p0, p1, p2, p3, chan_ref, msg_ref, out, gs):
        q = lax.axis_index("freq")
        pair = p0[...].astype(F32) + p1[...].astype(F32)
        new_chan = pair + (p2[...].astype(F32) + p3[...].astype(F32))
        chan_ref[...] = new_chan
        if ndev > rank:
            out[...] = jnp.zeros_like(out)
        channel_sums(new_chan.astype(BF16), held_spans, (buf0, buf1, buf2), [None] * 3, out)
        gs[...] = split_gram(new_chan, HIGHEST)
        side = packed_side(gs, q * 8, 4)
        out[:, freq_row:, :] = jnp.zeros((ndev, msg_rows - rows, LANES), F32)
        out[:, b_row : b_row + 4, :] = jnp.broadcast_to(side[None], (ndev, 4, LANES))
        msg_ref[...] = out[...].astype(BF16)

    new_chan, message = pl.pallas_call(
        images_kernel,
        out_shape=(jax.ShapeDtypeStruct((rank, chans), F32), msg),
        in_specs=[vmem] * 7,
        out_specs=(vmem, vmem),
        scratch_shapes=[pltpu.VMEM((ndev, msg_rows, LANES), F32), pltpu.VMEM((rank, LANES), F32)],
        compiler_params=params,
        name="image_sums",
    )(*held, last, *parts)
    received = lax.all_to_all(message, ALL, 0, 0, tiled=True)

    def terms_kernel(
        rcv_ref, starts_ref, taper_ref, table_ref, summed_ref, gram_ref,
        terms_ref, system_ref, z_ref, y_ref, gs,
    ):
        gram_a = gather_rank(rcv_ref, z_ref, gs)
        system_ref[...] = gram_a * gram_ref[...]
        images = forward(windows(z_ref, y_ref, starts_ref) * taper_ref[...], table_ref[...])
        terms = jnp.sum(images * summed_ref[...], axis=0, keepdims=True) / SEGS
        terms = terms[:, :HALF] + terms[:, HALF:]
        for d in range(ndev):
            q = d % nq
            terms_ref[d] = terms[:, q * bins : (q + 1) * bins]

    terms, system = pl.pallas_call(
        terms_kernel,
        out_shape=(jax.ShapeDtypeStruct((ndev, 1, bins), F32), square),
        in_specs=[vmem, smem, vmem, vmem, vmem, vmem],
        out_specs=(vmem, vmem),
        scratch_shapes=[
            pltpu.VMEM((z_rows, LANES), F32),
            pltpu.VMEM((SEGS, 8, LANES), F32),
            pltpu.VMEM((rank, LANES), F32),
        ],
        compiler_params=params,
        name="frequency_terms",
    )(received, starts, taper, table, summed, gram_b)
    terms = lax.all_to_all(terms, ALL, 0, 0, tiled=True)
    inverse = inverse_of(system)

    def finish_kernel(terms_ref, inverse_ref, out_ref):
        gathered = terms_ref[:rank, 0, :]
        out_ref[...] = dot(inverse_ref[...], gathered, precision=HIGHEST)

    new_freq = pl.pallas_call(
        finish_kernel,
        out_shape=jax.ShapeDtypeStruct((rank, bins), F32),
        in_specs=[vmem, vmem],
        out_specs=vmem,
        compiler_params=params,
        name="frequency_solve",
    )(terms, inverse)
    return (new_chan.T, new_freq.T)


def solution(mesh):
    return jax.shard_map(
        body,
        mesh=mesh,
        in_specs=(P(("row", "col"), None), P(), P(), P(("row", "col"), None), P("freq", None)),
        out_specs=(P(("row", "col"), None), P("freq", None)),
        check_vma=False,
    )
```

```python
import jax
import jax.numpy as jnp
import numpy as np
from jax import lax
from jax.experimental import pallas as pl
from jax.experimental.pallas import tpu as pltpu
from jax.sharding import PartitionSpec as P

NW = 1024
HALF = NW // 2
SEGS = 32
LANES = 128
ALL = ("row", "col", "freq")
F32 = jnp.float32
BF16 = jnp.bfloat16
HIGHEST = lax.Precision.HIGHEST
VMEM_BYTES = 32 << 20
AHEAD = 8
WIDE = NW + LANES
WINDOWS = 3
FIRST_SEGS = 14
PIECE = 1536


def half_table():
    position = np.arange(HALF)
    phase = (np.outer(position, position) % NW) * (2.0 * np.pi / NW)
    table = np.concatenate([np.cos(phase), -np.sin(phase)], axis=1)
    return jnp.asarray(table.astype(np.float32)).astype(BF16)


def iota(shape, axis):
    return lax.broadcasted_iota(jnp.int32, shape, axis)


def dot(a, b, contract=((1,), (0,)), precision=None):
    return lax.dot_general(
        a, b, (contract, ((), ())), precision=precision, preferred_element_type=F32
    )


def spd_inverse(system):
    size = system.shape[0]
    system = jnp.concatenate([system, jnp.zeros((size, LANES - size), F32)], axis=1)
    rows, cols = iota((size, LANES), 0), iota((size, LANES), 1)
    for i in range(size):
        col = jnp.broadcast_to(system[:, i : i + 1], (size, LANES))
        pivot = 1.0 / col[i : i + 1]
        scaled = jnp.where(cols[:1] == i, pivot, system[i : i + 1] * pivot)
        cleared = jnp.where(cols == i, 0.0, system)
        system = jnp.where(rows == i, scaled, cleared - col * scaled)
    return system[:, :size]


def split_gram(factor):
    size = factor.shape[0]
    tiled = dot(factor, jnp.concatenate([factor] * 4, axis=0), ((1,), (1,)))
    high = tiled.astype(BF16).astype(F32)
    return jnp.where(iota((size, LANES), 1) // size % 2 == 0, high, tiled - high)


def join_rows(ref, group):
    value = ref[...]
    value = value + pltpu.roll(value, LANES - 32, 1)
    other = pltpu.roll(value, 64, 1)
    return jnp.where(iota(value.shape, 0) % group < group // 2, value, other)[:, :32]


def packed_side(ref, start, count):
    upper = ref[pl.ds(start, count), :]
    lower = ref[pl.ds(start + count, count), :]
    return jnp.where(iota((count, LANES), 1) < 64, upper, lower)


def window_base(start, samples):
    base = jnp.minimum(start // LANES, samples // LANES - WIDE // LANES)
    return base, start - base * LANES


def taper_of(win_ref, starts_ref, samples):
    length = jnp.zeros((SEGS, LANES), F32)
    offset = jnp.zeros((SEGS, LANES), jnp.int32)
    which = iota((SEGS, LANES), 0)
    for k in range(SEGS):
        length = jnp.where(which == k, win_ref[k].astype(F32), length)
        offset = jnp.where(which == k, window_base(starts_ref[k], samples)[1], offset)
    scale = 1.0 / jnp.sqrt(0.375 * length)
    pieces = []
    for j in range(WIDE // LANES):
        position = (iota((SEGS, LANES), 1) + j * LANES - offset).astype(F32)
        angle = jnp.pi * (position / length - 0.5)
        square = angle * angle
        value = 1.0 + square * (
            -1.0 / 2
            + square
            * (
                1.0 / 24
                + square
                * (
                    -1.0 / 720
                    + square
                    * (1.0 / 40320 + square * (-1.0 / 3628800 + square * (1.0 / 479001600)))
                )
            )
        )
        inside = (position >= 0.0) & (position < length)
        pieces.append(jnp.where(inside, value * value * scale, 0.0))
    return jnp.concatenate(pieces, axis=1)


def forward(samples, table):
    low, high = samples[:, :HALF], samples[:, HALF:NW]
    rest = samples[:, NW:]
    low = jnp.concatenate([low[:, : WIDE - NW] + rest, low[:, WIDE - NW :]], axis=1)
    both = jnp.concatenate([low + high, low - high], axis=0)
    top = both.astype(BF16)
    rest = (both - top.astype(F32)).astype(BF16)
    out = dot(jnp.concatenate([top, rest], axis=0), table)
    out = out[: 2 * SEGS] + out[2 * SEGS :]
    return jnp.where(iota((SEGS, NW), 1) % 2 == 0, out[:SEGS], out[SEGS:])


def body(signal, starts, win_len, chan_factor, freq_factor):
    mesh_size = {name: lax.axis_size(name) for name in ALL}
    nq = mesh_size["freq"]
    nc = mesh_size["row"] * mesh_size["col"]
    ndev = nq * nc
    chans, samples = signal.shape
    bins, rank = freq_factor.shape
    span = samples // nq
    rows = span // LANES
    total_rows = rows * nq
    b_row, w_row = rows + 1, rows + 5
    msg_rows = rows + 7
    pairs = 2 * SEGS
    wide_rows = WIDE // LANES
    first_spans = [(0, 12), (12, 12), (24, rows - 24)]
    assert rank == 32 and nq == 4 and bins == LANES and ndev >= rank and nc % 8 == 0
    assert span % LANES == 0 and msg_rows % 8 == 0

    vmem = pl.BlockSpec(memory_space=pltpu.VMEM)
    smem = pl.BlockSpec(memory_space=pltpu.SMEM)
    hbm = pl.BlockSpec(memory_space=pltpu.HBM)
    params = pltpu.CompilerParams(vmem_limit_bytes=VMEM_BYTES)
    table = half_table()
    pinned = [
        pltpu.with_memory_space_constraint(x, pltpu.HBM)
        for x in (signal, chan_factor.T, freq_factor.T, win_len, starts)
    ]
    msg = jax.ShapeDtypeStruct((ndev, msg_rows, LANES), BF16)
    square = jax.ShapeDtypeStruct((rank, rank), F32)

    def fetch(signal_ref, spans, bufs, sem, ahead=8):
        base = lax.axis_index("freq") * span
        copies = []
        for i, ((first, count), buf) in enumerate(zip(spans, bufs)):
            where = pl.multiple_of(base + first * LANES, LANES)
            source = signal_ref.at[:, pl.ds(where, count * LANES)]
            copies.append(pltpu.make_async_copy(source, buf, sem.at[i]))
        for copy in copies[:ahead]:
            copy.start()
        return copies

    def channel_sums(lhs, spans, bufs, copies, out_ref, ahead=8):
        for i, (first, count) in enumerate(spans):
            if copies[i] is not None:
                copies[i].wait()
                if i + ahead < len(copies):
                    copies[i + ahead].start()
            part = dot(lhs, bufs[i][...])
            for j in range(count):
                out_ref[:rank, first + j, :] = part[:, j * LANES : (j + 1) * LANES]

    def sums_kernel(
        signal_ref, chan_hbm, freq_hbm, win_hbm, starts_hbm, msg_ref, taper_ref,
        buf, sem, chan_ref, freq_ref, win_ref, starts_ref, small, out, gs,
    ):
        small_copies = [
            pltpu.make_async_copy(chan_hbm, chan_ref, small.at[0]),
            pltpu.make_async_copy(freq_hbm, freq_ref, small.at[1]),
            pltpu.make_async_copy(win_hbm, win_ref, small.at[2]),
            pltpu.make_async_copy(starts_hbm, starts_ref, small.at[3]),
        ]
        for copy in small_copies:
            copy.start()
        bufs = [buf.at[:, a * LANES : (a + n) * LANES] for a, n in first_spans]
        copies = fetch(signal_ref, first_spans, bufs, sem, AHEAD)
        q = lax.axis_index("freq")
        c = lax.axis_index("row") * mesh_size["col"] + lax.axis_index("col")
        if ndev > rank:
            out[...] = jnp.zeros_like(out)
        for copy in small_copies:
            copy.wait()
        taper_ref[...] = taper_of(win_ref, starts_ref, samples)
        chan_low = chan_ref[...]
        weights_low = freq_ref[...]
        out[:, rows, :] = jnp.zeros((ndev, LANES), F32)
        gs[0] = split_gram(chan_low)
        gs[1] = split_gram(weights_low)
        channel_sums(chan_low, first_spans, bufs, copies, out, AHEAD)
        side = packed_side(gs.at[0], q * 8, 4)
        out[:, b_row : b_row + 4, :] = jnp.broadcast_to(side[None], (ndev, 4, LANES))
        side = packed_side(gs.at[1], (c % 8) * 4, 2)
        out[:, w_row : w_row + 2, :] = jnp.broadcast_to(side[None], (ndev, 2, LANES))
        msg_ref[...] = out[...].astype(BF16)

    message, taper = pl.pallas_call(
        sums_kernel,
        out_shape=(msg, jax.ShapeDtypeStruct((SEGS, WIDE), F32)),
        in_specs=[hbm] * 5,
        out_specs=(vmem, vmem),
        scratch_shapes=[
            pltpu.VMEM((chans, span), BF16),
            pltpu.SemaphoreType.DMA((len(first_spans),)),
            pltpu.VMEM((rank, chans), BF16),
            pltpu.VMEM((rank, bins), BF16),
            pltpu.SMEM((SEGS,), jnp.int32),
            pltpu.SMEM((SEGS,), jnp.int32),
            pltpu.SemaphoreType.DMA((4,)),
            pltpu.VMEM((ndev, msg_rows, LANES), F32),
            pltpu.VMEM((2, rank, LANES), F32),
        ],
        compiler_params=params,
        name="channel_sums",
    )(*pinned)
    received = lax.all_to_all(message, ALL, 0, 0, tiled=True)

    def spectra_part(first, count, taper, system=None):
        width = 2 * bins

        extra = () if system is None else (system,)

        def kernel(signal_ref, starts_ref, taper_ref, table_ref, *rest):
            *system_ref, spec_ref = rest[: len(extra) + 1]
            *inverse_ref, win, in_sem, out, out_sem, local = rest[len(extra) + 1 :]
            q = lax.axis_index("freq")

            def window(k, slot, side):
                where, _ = window_base(starts_ref[first + k], samples)
                where = pl.multiple_of(where * LANES, LANES)
                return pltpu.make_async_copy(
                    signal_ref.at[:, pl.ds(where, WIDE)],
                    win.at[slot, side],
                    in_sem.at[slot, side],
                )

            def store(k, side):
                where = pl.multiple_of(k * width, LANES)
                return pltpu.make_async_copy(
                    out.at[side], spec_ref.at[:, pl.ds(where, width)], out_sem.at[side]
                )

            for k in range(WINDOWS):
                for side in range(2):
                    window(2 * k + side, k, side).start()
            sign = 1 - 2 * (iota((HALF, bins), 1) % 2)
            for z in range(2):
                columns = pl.ds(pl.multiple_of(z * HALF + q * bins, LANES), bins)
                part = table_ref[:, columns]
                lanes = slice(z * bins, (z + 1) * bins)
                local[:HALF, lanes] = part
                local[HALF:NW, lanes] = (part.astype(F32) * sign.astype(F32)).astype(BF16)
                local[NW:, lanes] = part[: WIDE - NW]
            if extra:
                inverse_ref[0][...] = spd_inverse(system_ref[0][...])

            def step(k, carry):
                slot = lax.rem(k, WINDOWS)
                segments = []
                for side in range(2):
                    window(2 * k + side, slot, side).wait()
                    taper_row = taper_ref[pl.ds(first + 2 * k + side, 1), :].astype(BF16)
                    segments.append(win[slot, side] * taper_row)
                product = dot(jnp.concatenate(segments, axis=0), local[...]).astype(BF16)
                for side in range(2):

                    @pl.when(k >= 1)
                    def _():
                        store(2 * k - 2 + side, side).wait()

                    out[side] = product[side * chans : (side + 1) * chans]
                    store(2 * k + side, side).start()

                @pl.when(k + WINDOWS < count // 2)
                def _():
                    for side in range(2):
                        window(2 * (k + WINDOWS) + side, slot, side).start()

                return carry

            lax.fori_loop(0, count // 2, step, 0)
            for side in range(2):
                store(count - 2 + side, side).wait()

        spectra, *inverse = pl.pallas_call(
            kernel,
            out_shape=(pltpu.HBM((chans, count * width), BF16),) + (square,) * len(extra),
            in_specs=[hbm, smem, vmem, vmem] + [vmem] * len(extra),
            out_specs=(hbm,) + (vmem,) * len(extra),
            scratch_shapes=[
                pltpu.VMEM((WINDOWS, 2, chans, WIDE), BF16),
                pltpu.SemaphoreType.DMA((WINDOWS, 2)),
                pltpu.VMEM((2, chans, width), BF16),
                pltpu.SemaphoreType.DMA((2,)),
                pltpu.VMEM((WIDE, width), BF16),
            ],
            compiler_params=params,
            name="spectra",
        )(pinned[0], starts, taper, table, *extra)
        return [pltpu.with_memory_space_constraint(spectra, pltpu.HBM)] + inverse

    (spectra0,) = spectra_part(0, FIRST_SEGS, taper)

    def summed_kernel(
        rcv_ref, starts_ref, taper_ref, table_ref, _,
        msg_ref, system_ref, gram_ref, z_ref, y_ref, gs, out,
    ):
        for q in range(nq):
            total = rcv_ref[q].astype(F32)
            for c in range(1, nc):
                total = total + rcv_ref[c * nq + q].astype(F32)
            z_ref[q * rows : (q + 1) * rows, :] = total[:rows]
            gs[8 * q : 8 * q + 4, :] = total[b_row : b_row + 4]
            gs[8 * q + 4 : 8 * q + 8, :] = total[b_row : b_row + 4]
        gram_b = join_rows(gs, 8)
        gram_ref[...] = gram_b
        for c in range(8):
            side = rcv_ref[c * nq].astype(F32)[w_row : w_row + 2]
            for q in range(1, nq):
                side = side + rcv_ref[c * nq + q].astype(F32)[w_row : w_row + 2]
            gs[4 * c : 4 * c + 2, :] = side
            gs[4 * c + 2 : 4 * c + 4, :] = side
        system_ref[...] = gram_b * join_rows(gs, 4)
        for k in range(SEGS):
            base, _ = window_base(starts_ref[k], samples)
            y_ref[k, :wide_rows, :] = z_ref[pl.ds(base, wide_rows), :]
        windows = jnp.concatenate([y_ref[:, j, :] for j in range(wide_rows)], axis=1)
        summed = forward(windows * taper_ref[...], table_ref[...])
        for q in range(nq):
            for z in range(2):
                lanes = slice(z * HALF + q * bins, z * HALF + (q + 1) * bins)
                out[:, z, :] = summed[:, lanes]
            piece = out[...].reshape(pairs, LANES).astype(BF16)
            for c in range(nc):
                msg_ref[c * nq + q] = piece

    message, system, gram_b = pl.pallas_call(
        summed_kernel,
        out_shape=(jax.ShapeDtypeStruct((ndev, pairs, LANES), BF16), square, square),
        in_specs=[vmem, smem, vmem, vmem, hbm],
        out_specs=(vmem,) * 3,
        scratch_shapes=[
            pltpu.VMEM((total_rows, LANES), F32),
            pltpu.VMEM((SEGS, 16, LANES), F32),
            pltpu.VMEM((rank, LANES), F32),
            pltpu.VMEM((SEGS, 2, LANES), F32),
        ],
        compiler_params=params,
        name="summed",
    )(received, starts, taper, table, spectra0)
    received = lax.all_to_all(message, ALL, 0, 0, tiled=True)

    spectra1, inverse = spectra_part(FIRST_SEGS, SEGS - FIRST_SEGS, taper, system)

    width = pairs * bins
    cut0 = FIRST_SEGS * 2 * bins
    pieces = []
    for source, start, stop in ((0, 0, cut0), (1, cut0, width)):
        for at in range(start, stop, PIECE):
            pieces.append((source, at - start, at, min(PIECE, stop - at)))

    def contract_kernel(
        spec0, spec1, rcv_ref, freq_ref, inverse_ref, part_ref, summed_ref, *rest
    ):
        held, (sem, out, weighted) = rest[: len(pieces)], rest[len(pieces) :]
        copies = []
        for i, (source, begin, _, size) in enumerate(pieces):
            spec = (spec0, spec1)[source].at[:, begin : begin + size]
            copies.append(pltpu.make_async_copy(spec, held[i], sem.at[i]))
            copies[i].start()
        out[...] = rcv_ref[:rank].astype(F32)
        weights = freq_ref[...].astype(F32) / SEGS
        for j in range(pairs):
            value = out[:, j, :]
            summed_ref[:, j * LANES : (j + 1) * LANES] = value
            value = value * weights
            high = value.astype(BF16)
            weighted[:rank, j * LANES : (j + 1) * LANES] = high
            weighted[rank:, j * LANES : (j + 1) * LANES] = (value - high.astype(F32)).astype(BF16)
        total = jnp.zeros((2 * rank, chans), F32)
        for i, (_, _, start, size) in enumerate(pieces):
            copies[i].wait()
            total = total + dot(weighted[:, start : start + size], held[i][...], ((1,), (1,)))
        total = total[:rank] + total[rank:]
        part_ref[...] = dot(inverse_ref[...], total, precision=HIGHEST)

    part, summed, *held = pl.pallas_call(
        contract_kernel,
        out_shape=(
            jax.ShapeDtypeStruct((rank, chans), F32),
            jax.ShapeDtypeStruct((rank, width), F32),
        )
        + tuple(jax.ShapeDtypeStruct((chans, piece[3]), BF16) for piece in pieces),
        in_specs=[hbm, hbm, vmem, vmem, vmem],
        out_specs=(vmem,) * (2 + len(pieces)),
        scratch_shapes=[
            pltpu.SemaphoreType.DMA((len(pieces),)),
            pltpu.VMEM((rank, pairs, LANES), F32),
            pltpu.VMEM((2 * rank, pairs * LANES), BF16),
        ],
        compiler_params=params,
        name="contraction",
    )(spectra0, spectra1, received, freq_factor.T, inverse)
    parts = [part] + [
        lax.ppermute(part, "freq", [(i, i ^ m) for i in range(nq)]) for m in range(1, nq)
    ]

    last_rows = rank + 8

    def images_kernel(p0, p1, p2, p3, summed_ref, *rest):
        held, (chan_ref, msg_ref) = rest[: len(pieces)], rest[len(pieces) :]
        pair = p0[...].astype(F32) + p1[...].astype(F32)
        new_chan = pair + (p2[...].astype(F32) + p3[...].astype(F32))
        chan_ref[...] = new_chan
        rounded = new_chan.astype(BF16)
        terms = jnp.zeros((rank, bins), F32)
        for i, (_, _, start, size) in enumerate(pieces):
            images = dot(rounded, held[i][...])
            for j in range(size // LANES):
                at = start + j * LANES
                terms = terms + images[:, j * LANES : (j + 1) * LANES] * summed_ref[:, at : at + LANES]
        repeated = jnp.concatenate([new_chan] * 4, axis=0)
        gram = dot(new_chan, repeated, ((1,), (1,)), HIGHEST)
        packed = jnp.zeros((8, LANES), F32)
        for m in range(4):
            packed = jnp.where(iota((8, LANES), 1) // 32 == m, gram[8 * m : 8 * m + 8], packed)
        message = jnp.concatenate([terms / SEGS, packed], axis=0)
        msg_ref[...] = jnp.broadcast_to(message[None], (nc, last_rows, LANES))

    new_chan, message = pl.pallas_call(
        images_kernel,
        out_shape=(
            jax.ShapeDtypeStruct((rank, chans), F32),
            jax.ShapeDtypeStruct((nc, last_rows, LANES), F32),
        ),
        in_specs=[vmem] * (5 + len(pieces)),
        out_specs=(vmem, vmem),
        compiler_params=params,
        name="images",
    )(*parts, summed, *held)
    received = lax.all_to_all(message, ("row", "col"), 0, 0, tiled=True)

    def finish_kernel(rcv_ref, gram_ref, out_ref):
        total = rcv_ref[0]
        for c in range(1, nc):
            total = total + rcv_ref[c]
        packed = total[rank:]
        gram_a = jnp.concatenate(
            [pltpu.roll(packed, (LANES - 32 * m) % LANES, 1)[:, :32] for m in range(4)], axis=0
        )
        inverse = spd_inverse(gram_a * gram_ref[...])
        out_ref[...] = dot(inverse, total[:rank], precision=HIGHEST)

    new_freq = pl.pallas_call(
        finish_kernel,
        out_shape=jax.ShapeDtypeStruct((rank, bins), F32),
        in_specs=[vmem, vmem],
        out_specs=vmem,
        compiler_params=params,
        name="frequency_solve",
    )(received, gram_b)
    return (new_chan.T, new_freq.T)


def solution(mesh):
    return jax.shard_map(
        body,
        mesh=mesh,
        in_specs=(P(("row", "col"), None), P(), P(), P(("row", "col"), None), P("freq", None)),
        out_specs=(P(("row", "col"), None), P("freq", None)),
        check_vma=False,
    )
```
